128 devices in a mesh: row: 64 (over z, y, x), col: 2 (over core).
Axes of the slice: x: 4, y: 4, z: 4, core: 2. Of those that a mesh axis runs over, the one named last changes fastest.
Arguments:
- inputs: bfloat16 [16384, 1024], P(('row', 'col')), may hold values from -6 to 6
- segment_ids: int32 [64, 256], P('row'), may hold values from 0 to 2, as said below
- routes: int32 [16384, 8], P(('row', 'col')), may hold values from 0 to 31, all different within a row; in each aligned block of 128 rows (0 to 127, 128 to 255, ...) at most 36 rows name the same one
- first_gain: bfloat16 [1024], replicated, may hold values from 0.5 to 1.5
- query_matrix: bfloat16 [1024, 1024], P('row', 'col'), may hold values from -0.1875 to 0.1875
- key_matrix: bfloat16 [1024, 512], P('row', 'col'), may hold values from -0.1875 to 0.1875
- value_matrix: bfloat16 [1024, 512], P('row', 'col'), may hold values from -0.1875 to 0.1875
- output_weight: bfloat16 [1024, 1024], P('col', 'row'), may hold values from -1.5 to 1.5
- second_gain: bfloat16 [1024], replicated, may hold values from 0.5 to 1.5
- router_weight: bfloat16 [1024, 32], replicated, may hold values from -0.375 to 0.375
- gate_weight: bfloat16 [128, 256, 512], P(('row', 'col')), may hold values from -0.1875 to 0.1875
- up_weight: bfloat16 [128, 256, 512], P(('row', 'col')), may hold values from -0.1875 to 0.1875
- down_weight: bfloat16 [128, 512, 256], P(('row', 'col')), may hold values from -0.5 to 0.5
- cotangent: bfloat16 [16384, 1024], P(('row', 'col')), may hold values from -6 to 6
Outputs:
- layer_out: bfloat16 [16384, 1024], P(('row', 'col'))
- input_grad: float32 [16384, 1024], P(('row', 'col'))
- first_gain_grad: float32 [1024], replicated
- query_grad: float32 [1024, 1024], P('row', 'col')
- key_grad: float32 [1024, 512], P('row', 'col')
- value_grad: float32 [1024, 512], P('row', 'col')
- output_grad: float32 [1024, 1024], P('col', 'row')
- second_gain_grad: float32 [1024], replicated
- router_grad: float32 [1024, 32], replicated
- gate_grad: float32 [128, 256, 512], P(('row', 'col'))
- up_grad: float32 [128, 256, 512], P(('row', 'col'))
- down_grad: float32 [128, 512, 256], P(('row', 'col'))
The draws below stay inside these ranges and needn't reach their ends.
Inputs may be any that keep to these rules, and one draw needn't show every extreme that they name: `segment_ids`: along each sequence the document number starts at 0 and steps up by one at most twice; the first document ends before position 56; a document that starts and ends inside a sequence has at least 200 positions; some sequence holds three documents. `routes`: each token names 8 different experts; among the 128 tokens of one device (aligned blocks of rows) no expert is named more than 36 times, a bound that some block reaches.
All inputs are finite; a program needn't handle non-finite values.
Results may differ from the reference program's by a relative error of at most 0.014.
The reference program's roundings to bfloat16 on the way count: a program that leaves them out, or rounds other values in their place, can miss the bound.
Values may be sent and summed in bfloat16 or wider, within the bound.
A program may use at most 128 MiB of HBM per device.

```python
import math
import jax
import jax.numpy as jnp
import numpy as np
from jax import lax

MODEL_WIDTH = 1024
QUERY_HEAD_COUNT = 16
KEY_VALUE_HEADS = 8
HEAD_SIZE = 64
FE = 512
TOP = 8
EXPERTS = 32
SEQ_LEN = 256
DOC_MIN = 200
SEQS = 64
TOKENS = 16384
TOK_DEV = 128
REPLICAS = 4
CAP = 36


def draw_segment_ids(key, part):
    first_key, second_key = jax.random.split(jax.random.fold_in(key, 17))
    first_end = jax.random.randint(first_key, (SEQS, 1), 1, SEQ_LEN - DOC_MIN, dtype=jnp.int32)
    span = jax.random.randint(second_key, (SEQS, 1), DOC_MIN, 3 * SEQ_LEN, dtype=jnp.int32)
    seq_number = jnp.arange(SEQS, dtype=jnp.int32)[:, None]
    span = jnp.where(seq_number == 0, DOC_MIN, span)
    position = jnp.arange(SEQ_LEN, dtype=jnp.int32)[None, :]
    return (position >= first_end).astype(jnp.int32) + (position >= first_end + span).astype(jnp.int32)


def steps_of(own_key, dims, shards, smallest, top_value):
    level, own = 1.0, jax.random.fold_in(own_key, 6)
    for dim, blocks in shards:
        heights = jnp.exp(jax.random.uniform(jax.random.fold_in(own, dim), (blocks,), jnp.float32, smallest / len(shards), top_value / len(shards)))
        level = level * jnp.repeat(heights, dims[dim] // blocks).reshape([-1 if axis == dim else 1 for axis in range(len(dims))])
    return level


def routed_block(own_key, own, number, rows, number_of, top, limit, slope):
    order = jax.random.permutation(own_key, number_of)
    crowded, usual = portions_of(number_of, rows * top, limit, slope, True), portions_of(number_of, rows * top, limit, slope, False)
    places = jnp.arange(number_of)

    def named(lengths, turn):
        used = int((lengths > 0).sum())
        fixed = max(1, used // 4)
        shifted = fixed + (places - fixed + turn * (used - fixed)) % max(1, number_of - fixed)
        return jnp.zeros((number_of,), jnp.int32).at[order[jnp.where(places < fixed, places, shifted)]].set(jnp.asarray(lengths, jnp.int32))

    lengths = jnp.where(number % 4 == 0, named(crowded, number // 4), named(usual, number - number // 4 - 1))
    mixed = jax.random.permutation(jax.random.fold_in(own, 3), number_of)
    giver, sink = mixed[0:number_of // 2 * 2:2], mixed[1:number_of // 2 * 2:2]
    margin = jnp.minimum(lengths[giver] - 1, limit - lengths[sink]) // 2
    margin = jnp.where((giver == order[0]) | (sink == order[0]) | (lengths[sink] == 0), 0, jnp.maximum(margin, 0))
    shifted = jax.random.randint(jax.random.fold_in(own, 4), (number_of // 2,), 0, 1 << 20) % (margin + 1)
    lengths = lengths.at[giver].add(-shifted).at[sink].add(shifted)
    items = jnp.searchsorted(jnp.cumsum(lengths), jnp.arange(rows * top), side="right").astype(jnp.int32)
    listing = items.reshape(top, rows).T
    listing = listing[jax.random.permutation(jax.random.fold_in(own, 1), rows)]
    turn = jax.random.randint(jax.random.fold_in(own, 2), (rows, 1), 0, top)
    return jnp.take_along_axis(listing, (jnp.arange(top)[None, :] + turn) % top, axis=1)


def portions_of(number_of, total, bound, slope, full):
    portions = [(1 << 20) // math.isqrt(rank ** slope) + 1 for rank in range(1, number_of + 1)]
    largest = bound if full else min(bound, max(-(-total // number_of), total * portions[0] // sum(portions)))
    least = 1 if total - largest >= number_of - 1 else 0
    counts, rest = [largest] + [least] * (number_of - 1), total - largest - least * (number_of - 1)
    while rest > 0:
        candidates = [i for i in range(1, number_of) if counts[i] < largest] or [i for i in range(1, number_of) if counts[i] < bound]
        whole, left = sum([portions[i] for i in candidates]), rest
        for i in candidates:
            addition = min(bound - counts[i], max(1, left * portions[i] // whole), rest)
            counts[i] = counts[i] + addition
            rest = rest - addition
    return np.array(counts)


def noise(own_key, dims, deviation, most, cuts=(), kind=jnp.bfloat16):
    drawn = jax.random.normal(own_key, dims, jnp.float32) * deviation
    if len(cuts) > 0:
        drawn = steps_of(own_key, dims, cuts, -0.22, 0.18) * drawn
    return jnp.clip(drawn, min=-most, max=most).astype(kind)


def setup_inputs(seed: int = 0) -> dict:
    splits = jax.random.split(jax.random.key(seed), 15)
    inputs = noise(splits[0], (TOKENS, MODEL_WIDTH), 1.0, 6.0, ((0, 128),))
    segment_ids = draw_segment_ids(jax.random.fold_in(splits[14], 71), 0)
    routes_keys = jax.random.split(jax.random.fold_in(splits[2], 1), TOKENS // TOK_DEV)
    routes_turns = jax.random.permutation(jax.random.fold_in(splits[2], 3), TOKENS // TOK_DEV)
    routes = jax.vmap(lambda own, number: routed_block(jax.random.fold_in(splits[2], 2), own, number, TOK_DEV, EXPERTS, TOP, CAP, 2))(routes_keys, routes_turns).reshape((TOKENS, TOP))
    first_gain = jnp.clip(1.0 + 0.1 * jax.random.normal(splits[3], (MODEL_WIDTH,), jnp.float32), 0.5, 1.5).astype(jnp.bfloat16)
    query_matrix = noise(splits[4], (MODEL_WIDTH, QUERY_HEAD_COUNT * HEAD_SIZE), MODEL_WIDTH ** -0.5, 0.1875, ((0, 64), (1, 2)))
    key_matrix = noise(splits[5], (MODEL_WIDTH, KEY_VALUE_HEADS * HEAD_SIZE), MODEL_WIDTH ** -0.5, 0.1875, ((0, 64), (1, 2)))
    value_matrix = noise(splits[6], (MODEL_WIDTH, KEY_VALUE_HEADS * HEAD_SIZE), MODEL_WIDTH ** -0.5, 0.1875, ((0, 64), (1, 2)))
    output_weight = noise(splits[7], (QUERY_HEAD_COUNT * HEAD_SIZE, MODEL_WIDTH), (QUERY_HEAD_COUNT * HEAD_SIZE // 64) ** -0.5, 1.5, ((0, 2), (1, 64)))
    second_gain = jnp.clip(1.0 + 0.1 * jax.random.normal(splits[8], (MODEL_WIDTH,), jnp.float32), 0.5, 1.5).astype(jnp.bfloat16)
    router_weight = noise(splits[9], (MODEL_WIDTH, EXPERTS), (MODEL_WIDTH // 4) ** -0.5, 0.375)
    gate_weight = noise(splits[10], (REPLICAS * EXPERTS, MODEL_WIDTH // REPLICAS, FE), MODEL_WIDTH ** -0.5, 0.1875, ((0, 128),))
    up_weight = noise(splits[11], (REPLICAS * EXPERTS, MODEL_WIDTH // REPLICAS, FE), MODEL_WIDTH ** -0.5, 0.1875, ((0, 128),))
    down_weight = noise(splits[12], (REPLICAS * EXPERTS, FE, MODEL_WIDTH // REPLICAS), (FE // 4) ** -0.5, 0.5, ((0, 128),))
    cotangent = noise(splits[13], (TOKENS, MODEL_WIDTH), 1.0, 6.0, ((0, 128),))
    return {"inputs": inputs, "segment_ids": segment_ids, "routes": routes, "first_gain": first_gain, "query_matrix": query_matrix, "key_matrix": key_matrix, "value_matrix": value_matrix, "output_weight": output_weight, "second_gain": second_gain, "router_weight": router_weight, "gate_weight": gate_weight, "up_weight": up_weight, "down_weight": down_weight, "cotangent": cotangent}


@jax.custom_vjp
def reduced_precision(v):
    return lax.optimization_barrier(v.astype(jnp.bfloat16)).astype(jnp.float32)

@jax.custom_vjp
def reduced_backward(v):
    return v

def low_keep(v):
    return (reduced_precision(v), None)

def low_pass(kept, grad):
    return (grad,)

def back_keep(v):
    return (v, None)

def back_low(kept, grad):
    return (reduced_precision(grad),)
reduced_precision.defvjp(low_keep, low_pass)
reduced_backward.defvjp(back_keep, back_low)
HIGH = lax.Precision.HIGHEST
EPS = 1e-06

def precise_product(left, right):
    return jnp.dot(left, right, precision=HIGH, preferred_element_type=jnp.float32)

def rms_norm(values, gain):
    return values * lax.rsqrt(lax.optimization_barrier(jnp.mean(values * values, axis=-1, keepdims=True)) + EPS) * gain

def whole_rows(stored):
    return stored.reshape(REPLICAS, EXPERTS, MODEL_WIDTH // REPLICAS, FE).transpose(1, 0, 2, 3).reshape(EXPERTS, MODEL_WIDTH, FE)

def whole_cols(stored):
    return stored.reshape(REPLICAS, EXPERTS, FE, MODEL_WIDTH // REPLICAS).transpose(1, 2, 0, 3).reshape(EXPERTS, FE, MODEL_WIDTH)

def attention_part(normalized_input, segs, query_matrix, key_matrix, value_matrix, output_weight):
    sequence_total = segs.shape[0]
    sequence_length = segs.shape[1]
    projected_queries = reduced_backward(reduced_precision(precise_product(normalized_input, query_matrix))).reshape(sequence_total, sequence_length, KEY_VALUE_HEADS, QUERY_HEAD_COUNT // KEY_VALUE_HEADS, HEAD_SIZE)
    projected_keys = reduced_backward(reduced_precision(precise_product(normalized_input, key_matrix))).reshape(sequence_total, sequence_length, KEY_VALUE_HEADS, HEAD_SIZE)
    projected_values = reduced_backward(reduced_precision(precise_product(normalized_input, value_matrix))).reshape(sequence_total, sequence_length, KEY_VALUE_HEADS, HEAD_SIZE)
    raw_scores = jnp.einsum('sqhgd,skhd->shgqk', projected_queries, projected_keys, precision=HIGH) * HEAD_SIZE ** (-0.5)
    raw_scores = reduced_backward(raw_scores)
    position = jnp.arange(sequence_length, dtype=jnp.int32)
    allowed = (segs[:, :, None] == segs[:, None, :]) & (position[None, :, None] >= position[None, None, :])
    masked = jnp.where(allowed[:, None, None, :, :], raw_scores, -1e+30)
    soft_probs = jax.nn.softmax(masked, axis=-1)
    context = jnp.einsum('shgqk,skhd->sqhgd', reduced_precision(soft_probs), projected_values, precision=HIGH)
    context = reduced_backward(reduced_precision(context.reshape(sequence_total * sequence_length, QUERY_HEAD_COUNT * HEAD_SIZE)))
    return reduced_backward(precise_product(context, output_weight))

def expert_part(normalized_input, route_block, mix_weights, gate_weight, up_weight, down_weight):
    token_count = normalized_input.shape[0]
    block_count = token_count // TOK_DEV
    route_flat = route_block.reshape(-1)
    onehot = (route_flat[:, None] == jnp.arange(EXPERTS, dtype=jnp.int32)[None, :]).astype(jnp.int32)
    running = jnp.cumsum(onehot.reshape(block_count, TOK_DEV * TOP, EXPERTS), axis=1).reshape(-1, EXPERTS)
    slot_index = lax.optimization_barrier(jnp.sum(onehot * running, axis=1)) - 1
    pair_index = jnp.arange(token_count * TOP, dtype=jnp.int32)
    block_index = pair_index // (TOK_DEV * TOP)
    place = route_flat * (block_count * CAP) + block_index * CAP + slot_index
    owner_token = jnp.zeros((EXPERTS * block_count * CAP,), jnp.int32).at[place].set(pair_index // TOP)
    expert_rows = reduced_backward(normalized_input[owner_token]).reshape(EXPERTS, block_count * CAP, MODEL_WIDTH)

    def one_expert(tensors):
        rows_here, gate_here, up_here, down_here = tensors
        gate_pre = reduced_backward(precise_product(rows_here, gate_here))
        up_pre = reduced_backward(precise_product(rows_here, up_here))
        activated = reduced_precision(jax.nn.silu(gate_pre) * up_pre)
        return reduced_backward(reduced_precision(precise_product(activated, down_here)))
    results = lax.map(jax.checkpoint(one_expert), (expert_rows, gate_weight, up_weight, down_weight))
    pair_out = results.reshape(-1, MODEL_WIDTH)[place].reshape(token_count, TOP, MODEL_WIDTH)
    return lax.optimization_barrier(jnp.sum(mix_weights[:, :, None] * pair_out, axis=1))

def layer(block_x, segs, route_block, first_gain, query_matrix, key_matrix, value_matrix, output_weight, second_gain, router_weight, gate_weight, up_weight, down_weight):
    normed_one = reduced_precision(rms_norm(block_x, first_gain))
    hidden = block_x + attention_part(normed_one, segs, query_matrix, key_matrix, value_matrix, output_weight)
    normed_two = reduced_precision(rms_norm(hidden, second_gain))
    logits = reduced_backward(precise_product(normed_two, router_weight))
    chosen = route_block[:, :, None] == jnp.arange(EXPERTS, dtype=jnp.int32)[None, None, :]
    picked = lax.optimization_barrier(jnp.sum(jnp.where(chosen, logits[:, None, :], 0.0), axis=-1))
    mix_weights = jax.nn.softmax(picked, axis=-1)
    return hidden + expert_part(normed_two, route_block, mix_weights, whole_rows(gate_weight), whole_rows(up_weight), whole_cols(down_weight))

def reference(inputs, segment_ids, routes, first_gain, query_matrix, key_matrix, value_matrix, output_weight, second_gain, router_weight, gate_weight, up_weight, down_weight, cotangent):
    params = tuple((tensor.astype(jnp.float32) for tensor in (first_gain, query_matrix, key_matrix, value_matrix, output_weight, second_gain, router_weight, gate_weight, up_weight, down_weight)))
    group_seqs = max((divisor for divisor in range(1, SEQS + 1) if SEQS % divisor == 0 and (divisor * SEQ_LEN <= 4096 or divisor == 1)))
    groups = SEQS // group_seqs
    rows_group = group_seqs * SEQ_LEN
    input_blocks = inputs.astype(jnp.float32).reshape(groups, rows_group, MODEL_WIDTH)
    segment_blocks = segment_ids.reshape(groups, group_seqs, SEQ_LEN)
    route_blocks = routes.reshape(groups, rows_group, TOP)
    cot_blocks = cotangent.astype(jnp.float32).reshape(groups, rows_group, MODEL_WIDTH)

    def step(carry, tensors):
        block_in, block_seg, block_route, block_cot = tensors

        def forward(block_x, *weights):
            return layer(block_x, block_seg, block_route, *weights)
        result, pullback = jax.vjp(forward, block_in, *params)
        grads = pullback(block_cot)
        summed = tuple((before_sum + added for before_sum, added in zip(carry, grads[1:])))
        return (summed, (result, grads[0]))
    initial = tuple((jnp.zeros_like(tensor) for tensor in params))
    totals, (results, input_grads) = lax.scan(step, initial, (input_blocks, segment_blocks, route_blocks, cot_blocks))
    return (results.reshape(TOKENS, MODEL_WIDTH).astype(jnp.bfloat16), input_grads.reshape(TOKENS, MODEL_WIDTH), totals[0], totals[1], totals[2], totals[3], totals[4], totals[5], totals[6], totals[7], totals[8], totals[9])
```

```python
import jax
import jax.numpy as jnp
from jax import lax
from jax.sharding import Mesh
from jax.sharding import PartitionSpec as P

QUERY_HEAD_COUNT = 16
KEY_VALUE_HEADS = 8
HEAD_SIZE = 64
TOP = 8
ROW = ("row_0", "row_1", "row_2")
ROW_COL = ("row_0", "row_1", "row_2", "col")
PLANE = ("row_1", "row_2", "col")
RING = "row_0"
SLOTS = 40
SPARE = 36

EPS = 1e-06
NEG_FILL = -1e30
F32 = jnp.float32
BF16 = jnp.bfloat16


def in_order(pieces, dim):
    lengths = list(pieces.shape[1:])
    lengths[dim] *= pieces.shape[0]
    return jnp.moveaxis(pieces, 0, dim).reshape(lengths)


def swap_pieces(pieces, axis):
    return lax.all_to_all(pieces, axis, split_axis=0, concat_axis=0, tiled=True)


def from_everyone(shard, axis):
    return swap_pieces(jnp.broadcast_to(shard, (lax.axis_size(axis), *shard.shape)), axis)


def gather_directly(shard, axis, dim):
    return in_order(from_everyone(shard, axis), dim)


def split_up(shard, dim, devices):
    before, after = (shard.shape[:dim], shard.shape[dim + 1 :])
    return jnp.moveaxis(shard.reshape(*before, devices, -1, *after), dim, 0)


def sum_at_owner(shard, axis, dim):
    return swap_pieces(split_up(shard, dim, lax.axis_size(axis)), axis).astype(F32).sum(axis=0)


def ahead(value, axis):
    n = lax.axis_size(axis)
    return lax.ppermute(value, axis, [(i, (i + 1) % n) for i in range(n)])


def behind(value, axis):
    n = lax.axis_size(axis)
    return lax.ppermute(value, axis, [(i, (i - 1) % n) for i in range(n)])


def ring_gather(block, axis):
    me = lax.axis_index(axis)
    half = block.shape[1] // 2
    previous = ahead(block, axis)
    following = behind(block, axis)
    far = jnp.concatenate(
        [ahead(previous[:, :half], axis), behind(following[:, half:], axis)], axis=1
    )
    whole = jnp.zeros((block.shape[0], 4, *block.shape[1:]), block.dtype)
    for step, piece in ((0, block), (3, previous), (1, following), (2, far)):
        whole = lax.dynamic_update_slice_in_dim(whole, piece[:, None], (me + step) % 4, 1)
    return whole


def ring_reduce(total, axis):
    me = lax.axis_index(axis)
    half = total.shape[2] // 2

    def piece(step):
        return lax.dynamic_index_in_dim(total, (me + step) % 4, 1, keepdims=False)

    far, following, previous = piece(2), piece(1), piece(3)
    far_low = ahead(far[:, :half].astype(BF16), axis)
    far_high = behind(far[:, half:].astype(BF16), axis)
    following = jnp.concatenate(
        [following[:, :half] + far_low.astype(F32), following[:, half:]], axis=1
    )
    previous = jnp.concatenate(
        [previous[:, :half], previous[:, half:] + far_high.astype(F32)], axis=1
    )
    return (
        piece(0)
        + ahead(following.astype(BF16), axis).astype(F32)
        + behind(previous.astype(BF16), axis).astype(F32)
    )


def filled_up(lines, devices):
    spare = -lines.shape[0] % devices
    if not spare:
        return lines
    return jnp.concatenate([lines, jnp.zeros((spare, *lines.shape[1:]), lines.dtype)])


def whole_of(shard, axes, dim):
    far, near = axes
    pieces = from_everyone(from_everyone(shard, far), near)
    return in_order(pieces.swapaxes(0, 1).reshape(-1, *shard.shape), dim)


def sum_by_axis(shard, axes, dim):
    far, near = axes
    pieces = split_up(shard, dim, lax.axis_size(far))
    nearer = sum_at_owner(pieces, near, dim + 1)
    return swap_pieces(nearer, far).sum(axis=0)


def sum_by_parts(shard, axes):
    padded = filled_up(shard, lax.axis_size(axes[0]) * lax.axis_size(axes[1]))
    whole = whole_of(sum_by_axis(padded, axes, 0), axes, 0)
    return lax.slice_in_dim(whole, 0, len(shard)).reshape(shard.shape)


def in_one(arrays, axis):
    ravelled, at, gathered = (jnp.concatenate([a.reshape(-1) for a in arrays]), 0, [])
    total = sum_by_parts(ravelled, axis)
    for a in arrays:
        gathered.append(total[at : at + a.size].reshape(a.shape))
        at += a.size
    return tuple(gathered)


def rms_scale(values):
    return lax.rsqrt(jnp.mean(values * values, axis=-1, keepdims=True) + EPS)


def norm_back(grad_normed, values, inverse, gain):
    normed_unit = values * inverse
    scaled = grad_normed * gain
    grad_values = inverse * (
        scaled - normed_unit * jnp.mean(scaled * normed_unit, axis=-1, keepdims=True)
    )
    grad_gain = jnp.sum(grad_normed * normed_unit, axis=0)
    return (grad_values, grad_gain)


def times(left, right):
    return jnp.dot(left, right, preferred_element_type=F32)


def contract_rows(left, right):
    return lax.dot_general(left, right, (((0,), (0,)), ((), ())), preferred_element_type=F32)


def contract_cols(left, right):
    return lax.dot_general(left, right, (((1,), (1,)), ((), ())), preferred_element_type=F32)


def two_terms(values):
    high = lax.reduce_precision(values, 8, 7)
    return high.astype(BF16), (values - high).astype(BF16)


def with_scalars(rows, scalars):
    high, low = two_terms(scalars)
    line = jnp.pad(
        jnp.concatenate([jnp.pad(high, ((0, 0), (0, 128 - SLOTS))), low], axis=1),
        ((0, 0), (0, rows.shape[2] - 128 - SLOTS)),
    )
    at = jnp.arange(SLOTS)[None, :, None]
    return jnp.where(at == SPARE, line[:, None, :], rows)


def scalars_of(rows):
    line = rows[:, SPARE, :256].astype(F32)
    return line[:, :SLOTS] + line[:, 128 : 128 + SLOTS]


def shards(
    inputs,
    segment_ids,
    routes,
    first_gain,
    query_matrix,
    key_matrix,
    value_matrix,
    output_weight,
    second_gain,
    router_weight,
    gate_weight,
    up_weight,
    down_weight,
    cotangent,
):
    tokens_here, model_dim = inputs.shape
    group = QUERY_HEAD_COUNT // KEY_VALUE_HEADS
    score_scale = HEAD_SIZE ** (-0.5)
    experts = router_weight.shape[1]
    hidden_units = gate_weight.shape[2]

    blocks = jnp.stack([gate_weight[0], up_weight[0], down_weight[0].T])
    whole_weights = ring_gather(blocks, RING).reshape(3, model_dim, hidden_units)
    full_gate, full_up, full_down_t = whole_weights[0], whole_weights[1], whole_weights[2]

    inputs_float = inputs.astype(F32)
    inverse_one = rms_scale(inputs_float)
    gain_one = first_gain.astype(F32)
    normed_one = (inputs_float * inverse_one * gain_one).astype(BF16)
    seq_rows = gather_directly(normed_one, "col", 0)
    attention_weights = gather_directly(
        jnp.concatenate([query_matrix, key_matrix, value_matrix, output_weight.T], axis=1), ROW, 0
    )
    query_cols, key_cols = query_matrix.shape[1], key_matrix.shape[1]
    full_qkv = attention_weights[:, : query_cols + 2 * key_cols]
    full_output_t = attention_weights[:, query_cols + 2 * key_cols :]

    expert_ids = jnp.arange(experts, dtype=jnp.int32)
    chosen = jnp.any(routes[:, :, None] == expert_ids[None, None, :], axis=1)
    token = jnp.arange(tokens_here)
    rank = times((token[:, None] > token[None, :]).astype(BF16), chosen.astype(BF16))
    place = jnp.where(chosen, rank, -1.0).T
    selected = place[:, None, :] == jnp.arange(SLOTS, dtype=F32)[None, :, None]
    select = selected.astype(BF16).reshape(experts * SLOTS, tokens_here)

    def to_experts(rows):
        return swap_pieces(rows, PLANE)

    grad_sent = times(select, cotangent).astype(BF16).reshape(experts, SLOTS, model_dim)
    grad_rows_in = to_experts(grad_sent).reshape(experts * SLOTS, model_dim)

    length = seq_rows.shape[0]
    kv_heads = key_cols // HEAD_SIZE
    projected = times(seq_rows, full_qkv).astype(BF16)
    query_heads = projected[:, :query_cols].reshape(length, kv_heads, group, HEAD_SIZE)
    key_heads = projected[:, query_cols : query_cols + key_cols].reshape(
        length, kv_heads, HEAD_SIZE
    )
    value_heads = projected[:, query_cols + key_cols :].reshape(length, kv_heads, HEAD_SIZE)
    segment_row = segment_ids[0]
    position = jnp.arange(length, dtype=jnp.int32)
    allowed = (segment_row[:, None] == segment_row[None, :]) & (
        position[:, None] >= position[None, :]
    )

    def masked_scores():
        raw_scores = (
            jnp.einsum("qhgd,khd->hgqk", query_heads, key_heads, preferred_element_type=F32)
            * score_scale
        )
        return jnp.where(allowed, raw_scores, NEG_FILL)

    scores = masked_scores()
    row_max = jnp.max(scores, axis=-1, keepdims=True)
    exponent = jnp.exp(scores - row_max)
    row_total = jnp.sum(exponent, axis=-1, keepdims=True)
    attention_probs = exponent / row_total
    log_total = row_max + jnp.log(row_total)
    context = (
        jnp.einsum(
            "hgqk,khd->qhgd",
            attention_probs.astype(BF16),
            value_heads,
            preferred_element_type=F32,
        )
        .reshape(length, -1)
        .astype(BF16)
    )
    partial_value = contract_cols(context, full_output_t)
    hidden = inputs_float + sum_at_owner(partial_value, "col", 0)
    inverse_two = rms_scale(hidden)
    gain_two = second_gain.astype(F32)
    normed_two = (hidden * inverse_two * gain_two).astype(BF16)

    logits = jnp.where(chosen, times(normed_two, router_weight), NEG_FILL)
    raised = jnp.where(chosen, jnp.exp(logits - jnp.max(logits, axis=-1, keepdims=True)), 0.0)
    mix = raised / jnp.sum(raised, axis=-1, keepdims=True)
    mix_by_slot = jnp.where(selected, mix.T[:, None, :], 0.0)

    sent = times(select, normed_two).astype(BF16).reshape(experts, SLOTS, model_dim)
    arrived = to_experts(with_scalars(sent, mix_by_slot.sum(axis=-1)))
    received = arrived.reshape(experts * SLOTS, model_dim)
    mix_in = scalars_of(arrived).reshape(experts * SLOTS, 1)
    gate_pre = times(received, full_gate)
    up_pre = times(received, full_up)
    sigmoid_gate = jax.nn.sigmoid(gate_pre)
    silu_gate = gate_pre * sigmoid_gate
    activated = (silu_gate * up_pre).astype(BF16)
    grad_pair = (mix_in * grad_rows_in.astype(F32)).astype(BF16)
    grad_act = times(grad_pair, full_down_t)
    grad_gate_pre = (
        grad_act * up_pre * sigmoid_gate * (1.0 + gate_pre * (1.0 - sigmoid_gate))
    ).astype(BF16)
    grad_up_pre = (grad_act * silu_gate).astype(BF16)
    grad_received = contract_cols(grad_gate_pre, full_gate) + contract_cols(grad_up_pre, full_up)
    expert_out = contract_cols(activated, full_down_t).astype(BF16)
    grad_mix_out = jnp.sum(grad_rows_in.astype(F32) * expert_out.astype(F32), axis=-1)
    grad_back = to_experts(
        with_scalars(
            grad_received.astype(BF16).reshape(experts, SLOTS, model_dim),
            grad_mix_out.reshape(experts, SLOTS),
        )
    )
    expert_out, grad_back = lax.optimization_barrier((expert_out, grad_back))
    out_back = to_experts(expert_out.reshape(experts, SLOTS, model_dim)).reshape(
        experts * SLOTS, model_dim
    )

    expert_totals = jnp.stack(
        [
            contract_rows(received, grad_gate_pre),
            contract_rows(received, grad_up_pre),
            contract_rows(grad_pair, activated),
        ]
    ).reshape(3, 4, model_dim // 4, hidden_units)
    expert_grads = ring_reduce(expert_totals, RING)
    gate_grad = expert_grads[0][None]
    up_grad = expert_grads[1][None]
    down_grad = expert_grads[2].T[None]

    grad_layer = cotangent.astype(F32)
    grad_mix = jnp.sum(jnp.where(selected, scalars_of(grad_back)[:, :, None], 0.0), axis=1).T
    grad_picked = mix * (grad_mix - jnp.sum(mix * grad_mix, axis=-1, keepdims=True))
    grad_logits = grad_picked.astype(BF16)
    grad_from_experts = contract_rows(select, grad_back.reshape(experts * SLOTS, model_dim))
    grad_normed_two = grad_from_experts + contract_cols(grad_logits, router_weight)
    grad_hidden_norm, gain_two_term = norm_back(grad_normed_two, hidden, inverse_two, gain_two)
    grad_hidden = grad_layer + grad_hidden_norm
    router_term = contract_rows(normed_two, grad_logits)
    second_gain_grad, router_grad = in_one((gain_two_term, router_term), (ROW, "col"))

    grad_seq = gather_directly(grad_hidden.astype(BF16), "col", 0)
    grad_context = times(grad_seq, full_output_t).astype(BF16)
    grad_ctx_heads = grad_context.reshape(length, kv_heads, group, HEAD_SIZE)
    probs_again = jnp.exp(masked_scores() - log_total)
    grad_value_rows = (
        jnp.einsum(
            "hgqk,qhgd->khd",
            probs_again.astype(BF16),
            grad_ctx_heads,
            preferred_element_type=F32,
        )
        .reshape(length, -1)
        .astype(BF16)
    )
    grad_probs = jnp.einsum("qhgd,khd->hgqk", grad_ctx_heads, value_heads, preferred_element_type=F32)
    grad_scores = (
        probs_again * (grad_probs - jnp.sum(grad_probs * probs_again, axis=-1, keepdims=True))
    ).astype(BF16)
    grad_query_rows = (
        (
            jnp.einsum("hgqk,khd->qhgd", grad_scores, key_heads, preferred_element_type=F32)
            * score_scale
        )
        .reshape(length, -1)
        .astype(BF16)
    )
    grad_key_rows = (
        (
            jnp.einsum("hgqk,qhgd->khd", grad_scores, query_heads, preferred_element_type=F32)
            * score_scale
        )
        .reshape(length, -1)
        .astype(BF16)
    )
    grad_proj = jnp.concatenate([grad_query_rows, grad_key_rows, grad_value_rows], axis=1)
    grad_seq_norm = contract_cols(grad_proj, full_qkv)
    grad_normed_one = sum_at_owner(grad_seq_norm.astype(BF16), "col", 0)
    grad_input_norm, gain_one_term = norm_back(grad_normed_one, inputs_float, inverse_one, gain_one)
    input_grad = grad_hidden + grad_input_norm

    def to_owner(total):
        rows = total.shape[0]
        ring_sum = ring_reduce(total.reshape(1, 4, rows // 4, -1), RING)[0]
        pieces = ring_sum.astype(BF16).reshape(16, rows // 64, -1)
        return swap_pieces(pieces, ("row_1", "row_2")).astype(F32).sum(axis=0)

    output_grad = to_owner(contract_rows(grad_seq, context)).T
    qkv_grad = to_owner(contract_rows(seq_rows, grad_proj))
    query_grad = qkv_grad[:, :query_cols]
    key_grad = qkv_grad[:, query_cols : query_cols + key_cols]
    value_grad = qkv_grad[:, query_cols + key_cols :]
    first_gain_grad = from_everyone(gain_one_term.reshape(8, -1), ROW_COL).sum(axis=0).reshape(-1)
    layer_weights = two_terms(mix_by_slot.reshape(experts * SLOTS, tokens_here))
    mixture = contract_rows(layer_weights[0], out_back) + contract_rows(layer_weights[1], out_back)
    layer_out = (hidden + mixture).astype(BF16)
    return (
        layer_out,
        input_grad,
        first_gain_grad,
        query_grad,
        key_grad,
        value_grad,
        output_grad,
        second_gain_grad,
        router_grad,
        gate_grad,
        up_grad,
        down_grad,
    )


def solution(mesh):
    torus = Mesh(
        mesh.devices.reshape(4, 4, 4, mesh.shape["col"]), ("row_0", "row_1", "row_2", "col")
    )
    return jax.shard_map(
        shards,
        mesh=torus,
        in_specs=(
            P(ROW_COL, None),
            P(ROW, None),
            P(ROW_COL, None),
            P(),
            P(ROW, "col"),
            P(ROW, "col"),
            P(ROW, "col"),
            P("col", ROW),
            P(),
            P(),
            P(ROW_COL, None, None),
            P(ROW_COL, None, None),
            P(ROW_COL, None, None),
            P(ROW_COL, None),
        ),
        out_specs=(
            P(ROW_COL, None),
            P(ROW_COL, None),
            P(),
            P(ROW, "col"),
            P(ROW, "col"),
            P(ROW, "col"),
            P("col", ROW),
            P(),
            P(),
            P(ROW_COL, None, None),
            P(ROW_COL, None, None),
            P(ROW_COL, None, None),
        ),
        check_vma=False,
    )
```
